32 devices in a mesh: row: 8 (over y, x, core), col: 4 (over z).
Axes of the slice: x: 2, y: 2, z: 4, core: 2. Of those that a mesh axis runs over, the one named last changes fastest.
Arguments:
- activations: bfloat16 [1024, 8192], P(None, 'row'), may hold values from -10 to 10
- cotangents: bfloat16 [1024, 8192], P(None, 'row'), may hold values from -10 to 10
- act_factor: bfloat16 [8192, 8192], P('row', 'col'), may hold values from -0.5 to 1.5
- grad_factor: bfloat16 [8192, 8192], P('row', 'col'), may hold values from -0.5 to 1.5
Outputs:
- act_updated: bfloat16 [8192, 8192], P('row', 'col')
- grad_updated: bfloat16 [8192, 8192], P('row', 'col')
The draws below stay inside these ranges and needn't reach their ends.
All inputs are finite; a program needn't handle non-finite values.
Results may differ from the reference program's by a relative error of at most 0.0057.
Values may be sent and summed in bfloat16 or wider, within the bound.
A program may use at most 128 MiB of HBM per device.

```python
import jax
import jax.numpy as jnp
from jax import lax

D = 8192
TOKENS = 1024


def factor_draw(key):
    first, second = jax.random.split(key)
    spread = jnp.clip(jax.random.normal(first, (D, D), jnp.float32), -4.0, 4.0)
    diag = jax.random.uniform(second, (D,), jnp.float32, 0.9, 1.1)
    unit = jnp.eye(D, dtype=jnp.float32)
    return unit * diag[None, :] + (1.0 - unit) * spread * (0.5 / jnp.sqrt(jnp.float32(D)))


def rows_draw(key):
    first, second = jax.random.split(key, 2)
    place = jnp.arange(TOKENS, dtype=jnp.float32) / jnp.float32(max(TOKENS - 1, 1))
    jitter = jax.random.uniform(second, (TOKENS,), jnp.float32)
    scale = 0.2 * jnp.power(10.0, 0.5 * place + 0.5 * jitter)
    base = jnp.clip(jax.random.normal(first, (TOKENS, D), jnp.float32), -4.0, 4.0)
    return base * scale[:, None]


def draw_activations(key, part):
    return rows_draw(jax.random.fold_in(key, 101)).astype(jnp.bfloat16)


def draw_cotangents(key, part):
    return rows_draw(jax.random.fold_in(key, 202)).astype(jnp.bfloat16)


def draw_act_factor(key, part):
    return factor_draw(jax.random.fold_in(key, 303)).astype(jnp.bfloat16)


def draw_grad_factor(key, part):
    return factor_draw(jax.random.fold_in(key, 404)).astype(jnp.bfloat16)


def setup_inputs(seed: int = 0) -> dict:
    keys = jax.random.split(jax.random.key(seed), 5)
    activations = draw_activations(jax.random.fold_in(keys[4], 71), 0)
    cotangents = draw_cotangents(jax.random.fold_in(keys[4], 71), 0)
    act_factor = draw_act_factor(jax.random.fold_in(keys[4], 71), 0)
    grad_factor = draw_grad_factor(jax.random.fold_in(keys[4], 71), 0)
    return {"activations": activations, "cotangents": cotangents, "act_factor": act_factor, "grad_factor": grad_factor}


keep_scale = 1.45
gram_scale = 0.5


def project(rows, factor):
    return jnp.dot(rows.astype(jnp.float32), factor.astype(jnp.float32), precision=lax.Precision.HIGHEST).astype(jnp.bfloat16)


def update(factor, projected, scale):
    factor32 = factor.astype(jnp.float32)
    proj32 = projected.astype(jnp.float32)
    image = jnp.dot(factor32, proj32.T, precision=lax.Precision.HIGHEST).astype(jnp.bfloat16)
    image = lax.optimization_barrier(image).astype(jnp.float32)
    change = jnp.dot(image, proj32, precision=lax.Precision.HIGHEST)
    return (keep_scale * factor32 - (gram_scale * scale / TOKENS) * change).astype(jnp.bfloat16)


def reference(activations, cotangents, act_factor, grad_factor):
    act_proj = project(activations, act_factor)
    grad_proj = project(cotangents, grad_factor)
    act_mean = jnp.sum(jnp.square(act_proj.astype(jnp.float32))) / (TOKENS * D)
    grad_mean = jnp.sum(jnp.square(grad_proj.astype(jnp.float32))) / (TOKENS * D)
    return update(act_factor, act_proj, grad_mean), update(grad_factor, grad_proj, act_mean)
```

```python
import functools

import jax
import jax.numpy as jnp
from jax import lax
from jax.experimental import pallas as pl
from jax.experimental.pallas import tpu as pltpu
from jax.sharding import PartitionSpec as P

keep_scale = 1.45
gram_scale = 0.5

CHUNKS = 2
PIECES = 4
BF16 = jnp.bfloat16
F32 = jnp.float32


def schedule(levels, units, pieces, half, tokens, rows, width):
    link, chip, latency, flops = 0.065e6, 0.25e6, 1.6, 0.8e9
    unit_bytes = tokens * width * 2
    piece_bytes = rows // pieces * tokens * 2
    free = {}
    arrive = {}

    def send(line, now, size, rate):
        begin = max(now, free.get(line, 0.0))
        free[line] = begin + size / rate
        return free[line] + latency

    stages = 2 * levels
    pending = {}
    done = {}
    for u in range(units):
        for k in range(stages + 1):
            pending["E", u, k] = [("E", u, k - 1)] if k else []
        pending["Z0", u] = [("E", u, stages)]
        pending["S", u] = [("Z0", u)]
        for r in range(pieces):
            pending["Z1", u, r] = [("Z0", u)]
            pending["Z2", u, r] = [("Z1", u, r)]
            pending["Z3", u, r] = [("Z2", u, r)]
    pending["M1",] = [("S", u) for u in range(units)]
    pending["M2",] = [("M1",)]
    first = range(units // 2)
    second = range(units // 2, units)
    pending["F0",] = [("M2",)] + [("Z3", u, r) for u in first for r in range(pieces)]
    for r in range(pieces):
        pending["F1", r] = [("M2",)] + [("Z3", u, r) for u in second]
    rank = {"E": 0, "M1": 1, "M2": 2, "Z1": 2, "Z2": 1, "Z0": 3, "S": 4, "Z3": 5, "F0": 6, "F1": 4}

    def weight(event):
        kind = event[0]
        if kind == "E" and event[2] == 0:
            return (3.5, event[1])
        return (rank[kind],) + tuple(event[1:])

    work = 2.0 * tokens * rows * width / flops
    cost = {"Z0": work, "F0": work * units / 2, "F1": work * units / 2 / pieces, "S": 1.0, "M1": 0.5, "M2": 0.5}
    now, order = 0.0, []
    while pending:
        ready = []
        for event, deps in pending.items():
            if any(d in pending for d in deps):
                continue
            at = max([arrive.get(event, 0.0)] + [done[d] for d in deps])
            ready.append((max(at, now), weight(event), event))
        at, _, event = min(ready)
        kind = event[0]
        spent = cost.get(kind, 0.3)
        if kind == "E":
            spent = work if event[2] == 0 else 0.4
        now = at + spent
        del pending[event]
        done[event] = now
        order.append(event)
        if kind == "E" and event[2] < stages:
            u, k = event[1:]
            level = k if k < levels else stages - 1 - k
            size = unit_bytes / 2 ** (level + 1)
            rate = chip if level == 0 else link
            arrive["E", u, k + 1] = send(("row", level), now, size, rate)
        elif kind == "Z0":
            for r in range(pieces):
                begin = now - spent * (1 - (r + 1) / pieces)
                arrive["Z1", event[1], r] = send("up", begin, piece_bytes, 0.047e6)
        elif kind == "Z1":
            arrive["Z2", event[1], event[2]] = send("cross", now, piece_bytes, 0.047e6)
        elif kind == "Z2":
            arrive["Z3", event[1], event[2]] = send("down", now, piece_bytes, 0.047e6)
        elif kind == "M1":
            arrive["M2",] = now + 6.0
    return order


def kernel(
    n_row, n_col, order, chunks, pieces,
    act_in, grad_in, act_k, grad_k, act_out, grad_out,
    x_v, k_v, part, proj, own, up_in, cross_in, image, squares, means, *rest,
):
    levels = n_row.bit_length() - 1
    landing = rest[:levels]
    (load_sem, store_sem, row_send, row_recv, in_send, out_send, up_recv, in_recv,
     mean_send, mean_recv) = rest[levels:]
    units, tokens, width = part.shape
    rows = k_v.shape[1]
    height = rows // pieces
    half = n_col // 2
    stages = 2 * levels
    row = lax.axis_index("row")
    col = lax.axis_index("col")

    def factor(u):
        return u // chunks

    def at(start, size, unit=16):
        return pl.ds(pl.multiple_of(start, unit), size)

    odd = lax.rem(row, 2)
    partner, mine = [], []
    for s in range(levels):
        near = 2**s
        far = 1 if s == 0 else 2 ** (levels - s)
        near_bit = lax.rem(lax.div(row, near), 2)
        far_bit = lax.rem(lax.div(row, far), 2)
        near_peer = row + near * (1 - 2 * near_bit)
        far_peer = row + far * (1 - 2 * far_bit)
        mine.append(near_bit + odd * (far_bit - near_bit))
        partner.append(near_peer + odd * (far_peer - near_peer))
    starts, sizes = [0], [tokens]
    for s in range(levels):
        sizes.append(sizes[s] // 2)
        starts.append(starts[s] + mine[s] * sizes[s + 1])
    away = [starts[s] + (1 - mine[s]) * sizes[s + 1] for s in range(levels)]

    low = 1 - lax.div(col, half)
    depth = low * col + (1 - low) * (n_col - 1 - col)
    inward = col + 2 * low - 1
    outward = col - 2 * low + 1
    inner = depth == half - 1
    not_end = depth > 0

    barrier = pltpu.get_barrier_semaphore()
    for s in range(levels):
        pl.semaphore_signal(
            barrier, inc=1, device_id={"row": partner[s]}, device_id_type=pl.DeviceIdType.MESH
        )
    for d in range(1, n_col):
        pl.semaphore_signal(
            barrier, inc=1, device_id={"col": lax.rem(col + d, n_col)},
            device_id_type=pl.DeviceIdType.MESH,
        )

    loads = []
    for f, (x, k) in enumerate(((act_in, act_k), (grad_in, grad_k))):
        loads.append((
            pltpu.make_async_copy(x, x_v.at[f], load_sem.at[f, 0]),
            pltpu.make_async_copy(k, k_v.at[f], load_sem.at[f, 1]),
        ))
    for pair in loads:
        for copy in pair:
            copy.start()

    def remote(src, dst, send_sem, recv_sem, **device):
        return pltpu.make_async_remote_copy(
            src_ref=src, dst_ref=dst, send_sem=send_sem, recv_sem=recv_sem,
            device_id=device, device_id_type=pl.DeviceIdType.MESH,
        )

    def scatter_copy(u, s):
        size = sizes[s + 1]
        return remote(
            part.at[u, at(away[s], size)], landing[s].at[u],
            row_send.at[u, s], row_recv.at[u, s], row=partner[s],
        )

    def gather_copy(u, s):
        here = proj.at[u, at(starts[s + 1], sizes[s + 1])]
        k = stages - 1 - s
        return remote(here, here, row_send.at[u, k], row_recv.at[u, k], row=partner[s])

    def gather_arrival(u, s):
        there = proj.at[u, at(away[s], sizes[s + 1])]
        k = stages - 1 - s
        return remote(there, there, row_send.at[u, k], row_recv.at[u, k], row=partner[s])

    def piece(r):
        return pl.ds(r * height if isinstance(r, int) else pl.multiple_of(r * height, height), height)

    def up_copy(u, r):
        return remote(own.at[u, piece(r)], up_in.at[u, piece(r)], in_send.at[u, r], up_recv.at[u, r], col=inward)

    def cross_copy(u, r):
        return remote(own.at[u, piece(r)], cross_in.at[u, piece(r)], in_send.at[u, r], in_recv.at[u, r], col=inward)

    def down_copy(u, r):
        return remote(image.at[u, piece(r)], image.at[u, piece(r)], out_send.at[u, r], in_recv.at[u, r], col=outward)

    def send_inward(u, r):
        @pl.when(inner)
        def _():
            cross_copy(u, r).start()

        if half > 1:
            @pl.when(jnp.logical_not(inner))
            def _():
                up_copy(u, r).start()

    def mean_copy(d):
        to = lax.rem(col + d, n_col)
        return remote(means.at[col], means.at[col], mean_send.at[d], mean_recv.at[d], col=to)

    def mean_arrival(d):
        source = lax.rem(col + n_col - d, n_col)
        return remote(means.at[source], means.at[source], mean_send.at[d], mean_recv.at[d], col=source)

    step = min(512, width)
    scale = [None, None]
    entered = [False]
    loaded = [False, False]
    outs = (act_out, grad_out)
    stores = []

    def add_part(u, s, start, size):
        offset = start - starts[s + 1]
        tile = min(size, 64)

        @pl.loop(0, size // tile)
        def _(i):
            a = at(start + i * tile, tile)
            b = at(offset + i * tile, tile)
            part[u, a, :] = (part[u, a, :].astype(F32) + landing[s][u, b, :].astype(F32)).astype(BF16)

    def run_e(u, k):
        f = factor(u)
        if k == 0:
            if not loaded[f]:
                loaded[f] = True
                for copy in loads[f]:
                    copy.wait()
            base = (u % chunks) * tokens
            size = sizes[1]
            other = away[0]
            keep = starts[1]
            for start in (other, keep):
                @pl.loop(0, width // step)
                def _(j, start=start):
                    c = at(j * step, step, step)
                    part[u, at(start, size), c] = jnp.dot(
                        x_v[f, at(base + start, size), :], k_v[f, :, c], preferred_element_type=F32
                    ).astype(BF16)
                if start is other:
                    if not entered[0]:
                        entered[0] = True
                        pl.semaphore_wait(barrier, levels + n_col - 1)
                    scatter_copy(u, 0).start()
        elif k < levels:
            scatter_copy(u, k - 1).wait_recv()
            add_part(u, k - 1, away[k], sizes[k + 1])
            scatter_copy(u, k).start()
            add_part(u, k - 1, starts[k + 1], sizes[k + 1])
        elif k == levels:
            scatter_copy(u, k - 1).wait_recv()
            a = at(starts[levels], sizes[levels])
            proj[u, a, :] = (
                part[u, a, :].astype(F32) + landing[levels - 1][u].astype(F32)
            ).astype(BF16)
            gather_copy(u, levels - 1).start()
        elif k < stages:
            s = stages - k
            gather_arrival(u, s).wait_recv()
            gather_copy(u, s - 1).start()
        else:
            gather_arrival(u, 0).wait_recv()

    def run_squares(u):
        f = factor(u)
        tile = min(64, tokens)

        @pl.loop(0, tokens // tile)
        def _(i):
            p = proj[u, at(i * tile, tile), :].astype(F32)
            squares[f] += jnp.sum(jnp.square(p).reshape(tile // 8, 8, width), axis=0)

    def run_z0(u):
        f = factor(u)
        block = min(256, tokens)

        @pl.loop(0, pieces)
        def _(r):
            @pl.loop(0, tokens // block)
            def _(j):
                c = at(j * block, block, block)
                own[u, piece(r), c] = lax.dot_general(
                    k_v[f, piece(r), :], proj[u, c, :], (((1,), (1,)), ((), ())),
                    preferred_element_type=F32,
                ).astype(BF16)

            @pl.when(depth == 0)
            def _():
                send_inward(u, r)

    def run_z1(u, r):
        @pl.when(not_end)
        def _():
            up_copy(u, r).wait_recv()
            a = piece(r)
            own[u, a, :] = (own[u, a, :].astype(F32) + up_in[u, a, :].astype(F32)).astype(BF16)
            send_inward(u, r)

    def run_z2(u, r):
        @pl.when(inner)
        def _():
            cross_copy(u, r).wait_recv()
            a = piece(r)
            image[u, a, :] = (own[u, a, :].astype(F32) + cross_in[u, a, :].astype(F32)).astype(BF16)

            @pl.when(not_end)
            def _():
                down_copy(u, r).start()

    def run_z3(u, r):
        @pl.when(jnp.logical_not(inner))
        def _():
            down_copy(u, r).wait_recv()

            @pl.when(not_end)
            def _():
                down_copy(u, r).start()

    def run_m1():
        for f in range(2):
            total = squares[f, :, :128]
            for j in range(1, width // 128):
                total = total + squares[f, :, j * 128 : (j + 1) * 128]
            means[col, f] = total
        for d in range(1, n_col):
            mean_copy(d).start()

    def run_m2():
        for d in range(1, n_col):
            mean_arrival(d).wait_recv()
        entries = chunks * tokens * width * n_col
        for f in range(2):
            total = means[0, f]
            for j in range(1, n_col):
                total = total + means[j, f]
            scale[1 - f] = gram_scale / (chunks * tokens) * (jnp.sum(total) / entries)

    def change(f, r):
        @pl.loop(0, width // step)
        def _(j):
            c = at(j * step, step, step)
            total = None
            for u in range(f * chunks, (f + 1) * chunks):
                term = jnp.dot(image[u, piece(r), :], proj[u, :, c], preferred_element_type=F32)
                total = term if total is None else total + term
            k_v[f, piece(r), c] = (
                keep_scale * k_v[f, piece(r), c].astype(F32) - scale[f] * total
            ).astype(BF16)

    def run_f(f, r):
        if f == 0:
            @pl.loop(0, pieces)
            def _(i):
                change(0, i)

            copy = pltpu.make_async_copy(k_v.at[0], outs[0], store_sem.at[pieces])
        else:
            change(1, r)
            copy = pltpu.make_async_copy(k_v.at[1, piece(r)], outs[1].at[piece(r)], store_sem.at[r])
        copy.start()
        stores.append(copy)

    squares[...] = jnp.zeros(squares.shape, F32)
    for event in order:
        kind = event[0]
        if kind == "S":
            run_squares(event[1])
        elif kind == "E":
            run_e(event[1], event[2])
        elif kind == "Z0":
            run_z0(event[1])
        elif kind == "Z1":
            run_z1(*event[1:])
        elif kind == "Z2":
            run_z2(*event[1:])
        elif kind == "Z3":
            run_z3(*event[1:])
        elif kind == "M1":
            run_m1()
        elif kind == "M2":
            run_m2()
        elif kind == "F0":
            run_f(0, None)
        else:
            run_f(1, event[1])

    for u in range(units):
        for s in range(levels):
            scatter_copy(u, s).wait_send()
            gather_copy(u, s).wait_send()

        @pl.loop(0, pieces)
        def _(r, u=u):
            cross_copy(u, r).wait_send()

            @pl.when(not_end)
            def _():
                down_copy(u, r).wait_send()
    for d in range(1, n_col):
        mean_copy(d).wait_send()
    for copy in stores:
        copy.wait()


def local(n_row, n_col, activations, cotangents, act_factor, grad_factor):
    rows, width = act_factor.shape
    tokens = activations.shape[0] // CHUNKS
    units = 2 * CHUNKS
    levels = n_row.bit_length() - 1
    order = schedule(levels, units, PIECES, n_col // 2, tokens, rows, width)
    dma = pltpu.SemaphoreType.DMA
    anywhere = pl.BlockSpec(memory_space=pl.ANY)
    return pl.pallas_call(
        functools.partial(kernel, n_row, n_col, order, CHUNKS, PIECES),
        out_shape=[jax.ShapeDtypeStruct((rows, width), BF16)] * 2,
        in_specs=[anywhere] * 4,
        out_specs=[anywhere] * 2,
        scratch_shapes=[
            pltpu.VMEM((2,) + activations.shape, BF16),
            pltpu.VMEM((2, rows, width), BF16),
            pltpu.VMEM((units, tokens, width), BF16),
            pltpu.VMEM((units, tokens, width), BF16),
            pltpu.VMEM((units, rows, tokens), BF16),
            pltpu.VMEM((units, rows, tokens), BF16),
            pltpu.VMEM((units, rows, tokens), BF16),
            pltpu.VMEM((units, rows, tokens), BF16),
            pltpu.VMEM((2, 8, width), F32),
            pltpu.VMEM((n_col, 2, 8, 128), F32),
        ]
        + [pltpu.VMEM((units, tokens >> (s + 1), width), BF16) for s in range(levels)]
        + [
            dma((2, 2)),
            dma((PIECES + 1,)),
            dma((units, 2 * levels)),
            dma((units, 2 * levels)),
            dma((units, PIECES)),
            dma((units, PIECES)),
            dma((units, PIECES)),
            dma((units, PIECES)),
            dma((n_col,)),
            dma((n_col,)),
        ],
        compiler_params=pltpu.CompilerParams(
            collective_id=0, has_side_effects=True, vmem_limit_bytes=67043328
        ),
    )(activations, cotangents, act_factor, grad_factor)


def solution(mesh):
    return jax.shard_map(
        functools.partial(local, mesh.shape["row"], mesh.shape["col"]),
        mesh=mesh,
        in_specs=(P(None, "row"), P(None, "row"), P("row", "col"), P("row", "col")),
        out_specs=(P("row", "col"), P("row", "col")),
        check_vma=False,
    )
```

```python
import functools

import jax
import jax.numpy as jnp
from jax import lax
from jax.experimental import pallas as pl
from jax.experimental.pallas import tpu as pltpu
from jax.sharding import PartitionSpec as P

keep_scale = 1.45
gram_scale = 0.5

CHUNKS = 2
PIECES = 4
WINDOW = 2
BF16 = jnp.bfloat16
F32 = jnp.float32


def schedule(levels, units, pieces, half, tokens, rows, width):
    link, chip, latency, flops = 0.065e6, 0.25e6, 1.6, 0.8e9
    unit_bytes = tokens * width * 2
    piece_bytes = rows // pieces * tokens * 2
    free = {}
    arrive = {}

    def send(line, now, size, rate):
        begin = max(now, free.get(line, 0.0))
        free[line] = begin + size / rate
        return free[line] + latency

    stages = 2 * levels
    pending = {}
    done = {}
    for u in range(units):
        for k in range(stages + 1):
            pending["E", u, k] = [("E", u, k - 1)] if k else []
        pending["Z0", u] = [("E", u, stages)]
        pending["S", u] = [("Z0", u)]
        for r in range(pieces):
            pending["Z1", u, r] = [("Z0", u)]
            pending["Z2", u, r] = [("Z1", u, r)]
            pending["Z3", u, r] = [("Z2", u, r)]
    pending["M1",] = [("S", u) for u in range(units)]
    pending["M2",] = [("M1",)]
    first = range(units // 2)
    second = range(units // 2, units)
    pending["F0",] = [("M2",)] + [("Z3", u, r) for u in first for r in range(pieces)]
    for r in range(pieces):
        pending["F1", r] = [("M2",)] + [("Z3", u, r) for u in second]
    rank = {"E": 0, "M1": 1, "M2": 2, "Z1": 2, "Z2": 1, "Z0": 3, "S": 4, "Z3": 5, "F0": 6, "F1": 4}

    def weight(event):
        kind = event[0]
        if kind == "E" and event[2] == 0:
            return (3.5, event[1])
        return (rank[kind],) + tuple(event[1:])

    work = 2.0 * tokens * rows * width / flops
    cost = {"Z0": work, "F0": work * units / 2, "F1": work * units / 2 / pieces, "S": 1.0, "M1": 0.5, "M2": 0.5}
    now, order = 0.0, []
    while pending:
        ready = []
        for event, deps in pending.items():
            if any(d in pending for d in deps):
                continue
            at = max([arrive.get(event, 0.0)] + [done[d] for d in deps])
            ready.append((max(at, now), weight(event), event))
        at, _, event = min(ready)
        kind = event[0]
        spent = cost.get(kind, 0.3)
        if kind == "E":
            spent = work if event[2] == 0 else 0.4
        now = at + spent
        del pending[event]
        done[event] = now
        order.append(event)
        if kind == "E" and event[2] < stages:
            u, k = event[1:]
            level = k if k < levels else stages - 1 - k
            size = unit_bytes / 2 ** (level + 1)
            rate = chip if level == 0 else link
            arrive["E", u, k + 1] = send(("row", level), now, size, rate)
        elif kind == "Z0":
            for r in range(pieces):
                begin = now - spent * (1 - (r + 1) / pieces)
                arrive["Z1", event[1], r] = send("up", begin, piece_bytes, 0.047e6)
        elif kind == "Z1":
            arrive["Z2", event[1], event[2]] = send("cross", now, piece_bytes, 0.047e6)
        elif kind == "Z2":
            arrive["Z3", event[1], event[2]] = send("down", now, piece_bytes, 0.047e6)
        elif kind == "M1":
            arrive["M2",] = now + 6.0
    return order


def kernel(
    n_row, n_col, order, chunks, pieces,
    act_in, grad_in, act_k, grad_k, act_out, grad_out,
    x_v, k_v, kept, proj, own, up, image, squares, means, *rest,
):
    levels = n_row.bit_length() - 1
    landing = rest[:levels]
    leaving = rest[levels : 2 * levels]
    (load_sem, store_sem, row_send, row_recv, in_send, out_send, up_recv, in_recv,
     mean_send, mean_recv) = rest[2 * levels :]
    units, tokens, width = proj.shape
    rows = k_v.shape[1]
    height = rows // pieces
    half = n_col // 2
    stages = 2 * levels
    row = lax.axis_index("row")
    col = lax.axis_index("col")

    def factor(u):
        return u // chunks

    def at(start, size, unit=16):
        return pl.ds(pl.multiple_of(start, unit), size)

    odd = lax.rem(row, 2)
    partner, mine = [], []
    for s in range(levels):
        near = 2**s
        far = 1 if s == 0 else 2 ** (levels - s)
        near_bit = lax.rem(lax.div(row, near), 2)
        far_bit = lax.rem(lax.div(row, far), 2)
        near_peer = row + near * (1 - 2 * near_bit)
        far_peer = row + far * (1 - 2 * far_bit)
        mine.append(near_bit + odd * (far_bit - near_bit))
        partner.append(near_peer + odd * (far_peer - near_peer))
    starts, sizes = [0], [tokens]
    for s in range(levels):
        sizes.append(sizes[s] // 2)
        starts.append(starts[s] + mine[s] * sizes[s + 1])
    away = [starts[s] + (1 - mine[s]) * sizes[s + 1] for s in range(levels)]

    low = 1 - lax.div(col, half)
    depth = low * col + (1 - low) * (n_col - 1 - col)
    inward = col + 2 * low - 1
    outward = col - 2 * low + 1
    inner = depth == half - 1
    not_end = depth > 0

    barrier = pltpu.get_barrier_semaphore()
    for s in range(levels):
        pl.semaphore_signal(
            barrier, inc=1, device_id={"row": partner[s]}, device_id_type=pl.DeviceIdType.MESH
        )
    for d in range(1, n_col):
        pl.semaphore_signal(
            barrier, inc=1, device_id={"col": lax.rem(col + d, n_col)},
            device_id_type=pl.DeviceIdType.MESH,
        )

    loads = []
    for f, (x, k) in enumerate(((act_in, act_k), (grad_in, grad_k))):
        loads.append((
            pltpu.make_async_copy(x, x_v.at[f], load_sem.at[f, 0]),
            pltpu.make_async_copy(k, k_v.at[f], load_sem.at[f, 1]),
        ))
    for pair in loads:
        for copy in pair:
            copy.start()

    def remote(src, dst, send_sem, recv_sem, **device):
        return pltpu.make_async_remote_copy(
            src_ref=src, dst_ref=dst, send_sem=send_sem, recv_sem=recv_sem,
            device_id=device, device_id_type=pl.DeviceIdType.MESH,
        )

    def scatter_copy(u, s):
        return remote(
            leaving[s].at[u], landing[s].at[u],
            row_send.at[u, s], row_recv.at[u, s], row=partner[s],
        )

    def gather_copy(u, s):
        here = proj.at[u, at(starts[s + 1], sizes[s + 1])]
        k = stages - 1 - s
        return remote(here, here, row_send.at[u, k], row_recv.at[u, k], row=partner[s])

    def gather_arrival(u, s):
        there = proj.at[u, at(away[s], sizes[s + 1])]
        k = stages - 1 - s
        return remote(there, there, row_send.at[u, k], row_recv.at[u, k], row=partner[s])

    def piece(r):
        return pl.ds(r * height if isinstance(r, int) else pl.multiple_of(r * height, height), height)

    def up_copy(u, r):
        return remote(up.at[u, piece(r)], up.at[u, piece(r)], in_send.at[u, r], up_recv.at[u, r], col=inward)

    def cross_copy(u, r):
        return remote(up.at[u, piece(r)], image.at[u, piece(r)], in_send.at[u, r], in_recv.at[u, r], col=inward)

    def down_copy(u, r):
        return remote(image.at[u, piece(r)], image.at[u, piece(r)], out_send.at[u, r], in_recv.at[u, r], col=outward)

    def send_inward(u, r):
        @pl.when(inner)
        def _():
            cross_copy(u, r).start()

        if half > 1:
            @pl.when(jnp.logical_not(inner))
            def _():
                up_copy(u, r).start()

    def mean_copy(d):
        to = lax.rem(col + d, n_col)
        return remote(means.at[col], means.at[col], mean_send.at[d], mean_recv.at[d], col=to)

    def mean_arrival(d):
        source = lax.rem(col + n_col - d, n_col)
        return remote(means.at[source], means.at[source], mean_send.at[d], mean_recv.at[d], col=source)

    step = min(512, width)
    scale = [None, None]
    entered = [False]
    loaded = [False, False]
    outs = (act_out, grad_out)
    stores = []
    paced = []

    def add_kept(u, s, start, size, into):
        inside = start - starts[1]
        offset = start - starts[s + 1]
        tile = min(size, 64)

        @pl.loop(0, size // tile)
        def _(i):
            a = at(inside + i * tile, tile)
            total = kept[u, a, :] + landing[s][u, at(offset + i * tile, tile), :].astype(F32)
            if into is None:
                kept[u, a, :] = total
            else:
                into[u, pl.ds(pl.multiple_of(i * tile, tile), tile), :] = total.astype(BF16)

    def run_e(u, k):
        f = factor(u)
        if k == 0:
            if not loaded[f]:
                loaded[f] = True
                for copy in loads[f]:
                    copy.wait()
            base = (u % chunks) * tokens
            size = sizes[1]
            other = away[0]
            keep = starts[1]
            for start in (other, keep):
                @pl.loop(0, width // step)
                def _(j, start=start):
                    c = at(j * step, step, step)
                    product = jnp.dot(
                        x_v[f, at(base + start, size), :], k_v[f, :, c], preferred_element_type=F32
                    )
                    if start is other:
                        leaving[0][u, :, c] = product.astype(BF16)
                    else:
                        kept[u, :, c] = product
                if start is other:
                    if not entered[0]:
                        entered[0] = True
                        pl.semaphore_wait(barrier, levels + n_col - 1)
                    scatter_copy(u, 0).start()
        elif k < levels:
            scatter_copy(u, k - 1).wait_recv()
            add_kept(u, k - 1, away[k], sizes[k + 1], leaving[k])
            scatter_copy(u, k).start()
            add_kept(u, k - 1, starts[k + 1], sizes[k + 1], None)
        elif k == levels:
            scatter_copy(u, k - 1).wait_recv()
            a = at(starts[levels], sizes[levels])
            inside = at(starts[levels] - starts[1], sizes[levels])
            proj[u, a, :] = (kept[u, inside, :] + landing[levels - 1][u].astype(F32)).astype(BF16)
            gather_copy(u, levels - 1).start()
        elif k < stages:
            s = stages - k
            gather_arrival(u, s).wait_recv()
            gather_copy(u, s - 1).start()
        else:
            gather_arrival(u, 0).wait_recv()

    def run_squares(u):
        f = factor(u)
        tile = min(64, tokens)

        @pl.loop(0, tokens // tile)
        def _(i):
            p = proj[u, at(i * tile, tile), :].astype(F32)
            squares[f] += jnp.sum(jnp.square(p).reshape(tile // 8, 8, width), axis=0)

    def run_z0(u):
        f = factor(u)
        block = min(256, tokens)

        @pl.loop(0, pieces)
        def _(r):
            @pl.loop(0, tokens // block)
            def _(j):
                c = at(j * block, block, block)
                product = lax.dot_general(
                    k_v[f, piece(r), :], proj[u, c, :], (((1,), (1,)), ((), ())),
                    preferred_element_type=F32,
                )

                @pl.when(not_end)
                def _():
                    own[u, piece(r), c] = product

                @pl.when(depth == 0)
                def _():
                    up[u, piece(r), c] = product.astype(BF16)

                    if half == 1:
                        own[u, piece(r), c] = product

    def run_z1(u, r):
        @pl.when(depth == 0)
        def _():
            if len(paced) >= WINDOW:
                cross_copy(*paced[-WINDOW]).wait_send()
            send_inward(u, r)

        paced.append((u, r))

        @pl.when(not_end)
        def _():
            up_copy(u, r).wait_recv()
            a = piece(r)
            total = own[u, a, :] + up[u, a, :].astype(F32)
            own[u, a, :] = total
            up[u, a, :] = total.astype(BF16)
            send_inward(u, r)

    def run_z2(u, r):
        @pl.when(inner)
        def _():
            cross_copy(u, r).wait_recv()
            a = piece(r)
            image[u, a, :] = (own[u, a, :] + image[u, a, :].astype(F32)).astype(BF16)

            @pl.when(not_end)
            def _():
                down_copy(u, r).start()

    def run_z3(u, r):
        if half > 2:
            @pl.when(jnp.logical_and(not_end, jnp.logical_not(inner)))
            def _():
                down_copy(u, r).wait_recv()
                down_copy(u, r).start()

    def run_m1():
        for f in range(2):
            total = squares[f, :, :128]
            for j in range(1, width // 128):
                total = total + squares[f, :, j * 128 : (j + 1) * 128]
            means[col, f] = total
        for d in range(1, n_col):
            mean_copy(d).start()

    def run_m2():
        for d in range(1, n_col):
            mean_arrival(d).wait_recv()
        entries = chunks * tokens * width * n_col
        for f in range(2):
            total = means[0, f]
            for j in range(1, n_col):
                total = total + means[j, f]
            scale[1 - f] = gram_scale / (chunks * tokens) * (jnp.sum(total) / entries)

    def change(f, r):
        if half > 1:
            @pl.when(depth == 0)
            def _():
                for u in range(f * chunks, (f + 1) * chunks):
                    down_copy(u, r).wait_recv()

        @pl.loop(0, width // step)
        def _(j):
            c = at(j * step, step, step)
            total = None
            for u in range(f * chunks, (f + 1) * chunks):
                term = jnp.dot(image[u, piece(r), :], proj[u, :, c], preferred_element_type=F32)
                total = term if total is None else total + term
            k_v[f, piece(r), c] = (
                keep_scale * k_v[f, piece(r), c].astype(F32) - scale[f] * total
            ).astype(BF16)

    def run_f(f, r):
        if f == 0:
            @pl.loop(0, pieces)
            def _(i):
                change(0, i)

            copy = pltpu.make_async_copy(k_v.at[0], outs[0], store_sem.at[pieces])
        else:
            change(1, r)
            copy = pltpu.make_async_copy(k_v.at[1, piece(r)], outs[1].at[piece(r)], store_sem.at[r])
        copy.start()
        stores.append(copy)

    squares[...] = jnp.zeros(squares.shape, F32)
    for event in order:
        kind = event[0]
        if kind == "S":
            run_squares(event[1])
        elif kind == "E":
            run_e(event[1], event[2])
        elif kind == "Z0":
            run_z0(event[1])
        elif kind == "Z1":
            run_z1(*event[1:])
        elif kind == "Z2":
            run_z2(*event[1:])
        elif kind == "Z3":
            run_z3(*event[1:])
        elif kind == "M1":
            run_m1()
        elif kind == "M2":
            run_m2()
        elif kind == "F0":
            run_f(0, None)
        else:
            run_f(1, event[1])

    for u in range(units):
        for s in range(levels):
            scatter_copy(u, s).wait_send()
            gather_copy(u, s).wait_send()

    for i, (u, r) in enumerate(paced):
        if i + WINDOW >= len(paced):
            cross_copy(u, r).wait_send()
        else:
            @pl.when(not_end)
            def _(u=u, r=r):
                cross_copy(u, r).wait_send()

        @pl.when(not_end)
        def _(u=u, r=r):
            down_copy(u, r).wait_send()
    for d in range(1, n_col):
        mean_copy(d).wait_send()
    for copy in stores:
        copy.wait()


def local(n_row, n_col, activations, cotangents, act_factor, grad_factor):
    rows, width = act_factor.shape
    tokens = activations.shape[0] // CHUNKS
    units = 2 * CHUNKS
    levels = n_row.bit_length() - 1
    order = schedule(levels, units, PIECES, n_col // 2, tokens, rows, width)
    dma = pltpu.SemaphoreType.DMA
    anywhere = pl.BlockSpec(memory_space=pl.ANY)
    return pl.pallas_call(
        functools.partial(kernel, n_row, n_col, order, CHUNKS, PIECES),
        out_shape=[jax.ShapeDtypeStruct((rows, width), BF16)] * 2,
        in_specs=[anywhere] * 4,
        out_specs=[anywhere] * 2,
        scratch_shapes=[
            pltpu.VMEM((2,) + activations.shape, BF16),
            pltpu.VMEM((2, rows, width), BF16),
            pltpu.VMEM((units, tokens // 2, width), F32),
            pltpu.VMEM((units, tokens, width), BF16),
            pltpu.VMEM((units, rows, tokens), F32),
            pltpu.VMEM((units, rows, tokens), BF16),
            pltpu.VMEM((units, rows, tokens), BF16),
            pltpu.VMEM((2, 8, width), F32),
            pltpu.VMEM((n_col, 2, 8, 128), F32),
        ]
        + [pltpu.VMEM((units, tokens >> (s + 1), width), BF16) for s in range(levels)] * 2
        + [
            dma((2, 2)),
            dma((PIECES + 1,)),
            dma((units, 2 * levels)),
            dma((units, 2 * levels)),
            dma((units, PIECES)),
            dma((units, PIECES)),
            dma((units, PIECES)),
            dma((units, PIECES)),
            dma((n_col,)),
            dma((n_col,)),
        ],
        compiler_params=pltpu.CompilerParams(
            collective_id=0, has_side_effects=True, vmem_limit_bytes=67043328
        ),
    )(activations, cotangents, act_factor, grad_factor)


def solution(mesh):
    return jax.shard_map(
        functools.partial(local, mesh.shape["row"], mesh.shape["col"]),
        mesh=mesh,
        in_specs=(P(None, "row"), P(None, "row"), P("row", "col"), P("row", "col")),
        out_specs=(P("row", "col"), P("row", "col")),
        check_vma=False,
    )
```

```python
import functools

import jax
import jax.numpy as jnp
from jax import lax
from jax.experimental import pallas as pl
from jax.experimental.pallas import tpu as pltpu
from jax.sharding import PartitionSpec as P

keep_scale = 1.45
gram_scale = 0.5

CHUNKS = 4
PIECES = 4
WINDOW = 2
BF16 = jnp.bfloat16
F32 = jnp.float32


def schedule(levels, units, pieces, half, tokens, rows, width):
    link, chip, latency, flops = 0.065e6, 0.25e6, 1.6, 0.8e9
    unit_bytes = tokens * width * 2
    piece_bytes = rows // pieces * tokens * 2
    free = {}
    arrive = {}

    def send(line, now, size, rate):
        begin = max(now, free.get(line, 0.0))
        free[line] = begin + size / rate
        return free[line] + latency

    stages = 2 * levels
    pending = {}
    done = {}
    for u in range(units):
        for k in range(stages + 1):
            pending["E", u, k] = [("E", u, k - 1)] if k else []
            if k == 1 and u >= 1:
                pending["E", u, k].append(("E", u - 1, 2))
            if k == 1 and u >= 2:
                pending["E", u, k].append(("E", u - 2, stages))
        pending["Z0", u] = [("E", u, stages)]
        pending["S", u] = [("Z0", u)]
        for r in range(pieces):
            pending["Z1", u, r] = [("Z0", u)]
            pending["Z2", u, r] = [("Z1", u, r)]
            pending["Z3", u, r] = [("Z2", u, r)]
    pending["M1",] = [("S", u) for u in range(units)]
    pending["M2",] = [("M1",)]
    first = range(units // 2)
    second = range(units // 2, units)
    pending["F0",] = [("M2",)] + [("Z3", u, r) for u in first for r in range(pieces)]
    for r in range(pieces):
        pending["F1", r] = [("M2",)] + [("Z3", u, r) for u in second]
    rank = {"E": 0, "M1": 1, "M2": 2, "Z1": 2, "Z2": 1, "Z0": 3, "S": 4, "Z3": 5, "F0": 6, "F1": 4}

    def weight(event):
        kind = event[0]
        if kind == "E" and event[2] == 0:
            return (3.5, event[1])
        return (rank[kind],) + tuple(event[1:])

    work = 2.0 * tokens * rows * width / flops
    cost = {"Z0": work, "F0": work * units / 2, "F1": work * units / 2 / pieces, "S": 1.0, "M1": 0.5, "M2": 0.5}
    now, order = 0.0, []
    while pending:
        ready = []
        for event, deps in pending.items():
            if any(d in pending for d in deps):
                continue
            at = max([arrive.get(event, 0.0)] + [done[d] for d in deps])
            ready.append((max(at, now), weight(event), event))
        at, _, event = min(ready)
        kind = event[0]
        spent = cost.get(kind, 0.3)
        if kind == "E":
            spent = work if event[2] == 0 else 0.4
        now = at + spent
        del pending[event]
        done[event] = now
        order.append(event)
        if kind == "E" and event[2] < stages:
            u, k = event[1:]
            level = k if k < levels else stages - 1 - k
            size = unit_bytes / 2 ** (level + 1)
            rate = chip if level == 0 else link
            arrive["E", u, k + 1] = send(("row", level), now, size, rate)
        elif kind == "Z0":
            for r in range(pieces):
                begin = now - spent * (1 - (r + 1) / pieces)
                arrive["Z1", event[1], r] = send("up", begin, piece_bytes, 0.047e6)
        elif kind == "Z1":
            arrive["Z2", event[1], event[2]] = send("cross", now, piece_bytes, 0.047e6)
        elif kind == "Z2":
            arrive["Z3", event[1], event[2]] = send("down", now, piece_bytes, 0.047e6)
        elif kind == "M1":
            arrive["M2",] = now + 6.0
    return order


def kernel(
    n_row, n_col, order, chunks, pieces,
    act_in, grad_in, act_k, grad_k, act_out, grad_out,
    x_v, k_v, kept, proj, own, up, image, squares, means, *rest,
):
    levels = n_row.bit_length() - 1
    landing = rest[:levels]
    leaving = rest[levels : 2 * levels]
    (load_sem, store_sem, row_send, row_recv, in_send, out_send, up_recv, in_recv,
     mean_send, mean_recv) = rest[2 * levels :]
    units, tokens, width = proj.shape
    rows = k_v.shape[1]
    height = rows // pieces
    half = n_col // 2
    stages = 2 * levels
    row = lax.axis_index("row")
    col = lax.axis_index("col")

    def factor(u):
        return u // chunks

    def at(start, size, unit=16):
        return pl.ds(pl.multiple_of(start, unit), size)

    odd = lax.rem(row, 2)
    partner, mine = [], []
    for s in range(levels):
        near = 2**s
        far = 1 if s == 0 else 2 ** (levels - s)
        near_bit = lax.rem(lax.div(row, near), 2)
        far_bit = lax.rem(lax.div(row, far), 2)
        near_peer = row + near * (1 - 2 * near_bit)
        far_peer = row + far * (1 - 2 * far_bit)
        mine.append(near_bit + odd * (far_bit - near_bit))
        partner.append(near_peer + odd * (far_peer - near_peer))
    starts, sizes = [0], [tokens]
    for s in range(levels):
        sizes.append(sizes[s] // 2)
        starts.append(starts[s] + mine[s] * sizes[s + 1])
    away = [starts[s] + (1 - mine[s]) * sizes[s + 1] for s in range(levels)]

    low = 1 - lax.div(col, half)
    depth = low * col + (1 - low) * (n_col - 1 - col)
    inward = col + 2 * low - 1
    outward = col - 2 * low + 1
    inner = depth == half - 1
    not_end = depth > 0

    barrier = pltpu.get_barrier_semaphore()
    for s in range(levels):
        pl.semaphore_signal(
            barrier, inc=1, device_id={"row": partner[s]}, device_id_type=pl.DeviceIdType.MESH
        )
    for d in range(1, n_col):
        pl.semaphore_signal(
            barrier, inc=1, device_id={"col": lax.rem(col + d, n_col)},
            device_id_type=pl.DeviceIdType.MESH,
        )

    loads = []
    for f, (x, k) in enumerate(((act_in, act_k), (grad_in, grad_k))):
        loads.append((
            pltpu.make_async_copy(x, x_v.at[f], load_sem.at[f, 0]),
            pltpu.make_async_copy(k, k_v.at[f], load_sem.at[f, 1]),
        ))
    for pair in loads:
        for copy in pair:
            copy.start()

    def remote(src, dst, send_sem, recv_sem, **device):
        return pltpu.make_async_remote_copy(
            src_ref=src, dst_ref=dst, send_sem=send_sem, recv_sem=recv_sem,
            device_id=device, device_id_type=pl.DeviceIdType.MESH,
        )

    def scatter_copy(u, s):
        return remote(
            leaving[s].at[u], landing[s].at[u],
            row_send.at[u, s], row_recv.at[u, s], row=partner[s],
        )

    def gather_copy(u, s):
        here = proj.at[u, at(starts[s + 1], sizes[s + 1])]
        k = stages - 1 - s
        return remote(here, here, row_send.at[u, k], row_recv.at[u, k], row=partner[s])

    def gather_arrival(u, s):
        there = proj.at[u, at(away[s], sizes[s + 1])]
        k = stages - 1 - s
        return remote(there, there, row_send.at[u, k], row_recv.at[u, k], row=partner[s])

    def piece(r):
        return pl.ds(r * height if isinstance(r, int) else pl.multiple_of(r * height, height), height)

    def up_copy(u, r):
        return remote(up.at[u, piece(r)], up.at[u, piece(r)], in_send.at[u, r], up_recv.at[u, r], col=inward)

    def cross_copy(u, r):
        return remote(up.at[u, piece(r)], image.at[u, piece(r)], in_send.at[u, r], in_recv.at[u, r], col=inward)

    def down_copy(u, r):
        return remote(image.at[u, piece(r)], image.at[u, piece(r)], out_send.at[u, r], in_recv.at[u, r], col=outward)

    def send_inward(u, r):
        @pl.when(inner)
        def _():
            cross_copy(u, r).start()

        if half > 1:
            @pl.when(jnp.logical_not(inner))
            def _():
                up_copy(u, r).start()

    def mean_copy(d):
        to = lax.rem(col + d, n_col)
        return remote(means.at[col], means.at[col], mean_send.at[d], mean_recv.at[d], col=to)

    def mean_arrival(d):
        source = lax.rem(col + n_col - d, n_col)
        return remote(means.at[source], means.at[source], mean_send.at[d], mean_recv.at[d], col=source)

    step = min(512, width)
    scale = [None, None]
    entered = [False]
    loaded = [False, False]
    outs = (act_out, grad_out)
    stores = []
    paced = []

    def add_kept(u, s, start, size, into):
        inside = start - starts[1]
        offset = start - starts[s + 1]
        tile = min(size, 64)

        @pl.loop(0, size // tile)
        def _(i):
            a = at(inside + i * tile, tile)
            total = kept[u, a, :] + landing[s][u, at(offset + i * tile, tile), :].astype(F32)
            if into is None:
                kept[u, a, :] = total
            else:
                into[u, pl.ds(pl.multiple_of(i * tile, tile), tile), :] = total.astype(BF16)

    def run_e(u, k):
        f = factor(u)
        if k == 0:
            if not loaded[f]:
                loaded[f] = True
                for copy in loads[f]:
                    copy.wait()
            base = (u % chunks) * tokens
            size = sizes[1]
            other = away[0]
            keep = starts[1]
            for start in (other, keep):
                @pl.loop(0, width // step)
                def _(j, start=start):
                    c = at(j * step, step, step)
                    product = jnp.dot(
                        x_v[f, at(base + start, size), :], k_v[f, :, c], preferred_element_type=F32
                    )
                    if start is other:
                        leaving[0][u, :, c] = product.astype(BF16)
                    else:
                        kept[u, :, c] = product
                if start is other:
                    if not entered[0]:
                        entered[0] = True
                        pl.semaphore_wait(barrier, levels + n_col - 1)
                    scatter_copy(u, 0).start()
        elif k < levels:
            scatter_copy(u, k - 1).wait_recv()
            add_kept(u, k - 1, away[k], sizes[k + 1], leaving[k])
            scatter_copy(u, k).start()
            add_kept(u, k - 1, starts[k + 1], sizes[k + 1], None)
        elif k == levels:
            scatter_copy(u, k - 1).wait_recv()
            a = at(starts[levels], sizes[levels])
            inside = at(starts[levels] - starts[1], sizes[levels])
            proj[u, a, :] = (kept[u, inside, :] + landing[levels - 1][u].astype(F32)).astype(BF16)
            gather_copy(u, levels - 1).start()
        elif k < stages:
            s = stages - k
            gather_arrival(u, s).wait_recv()
            gather_copy(u, s - 1).start()
        else:
            gather_arrival(u, 0).wait_recv()

    def run_squares(u):
        f = factor(u)
        tile = min(64, tokens)

        @pl.loop(0, tokens // tile)
        def _(i):
            p = proj[u, at(i * tile, tile), :].astype(F32)
            squares[f] += jnp.sum(jnp.square(p).reshape(tile // 8, 8, width), axis=0)

    def run_z0(u):
        f = factor(u)
        block = min(256, tokens)

        @pl.loop(0, pieces)
        def _(r):
            @pl.loop(0, tokens // block)
            def _(j):
                c = at(j * block, block, block)
                product = lax.dot_general(
                    k_v[f, piece(r), :], proj[u, c, :], (((1,), (1,)), ((), ())),
                    preferred_element_type=F32,
                )

                @pl.when(not_end)
                def _():
                    own[u, piece(r), c] = product

                @pl.when(depth == 0)
                def _():
                    up[u, piece(r), c] = product.astype(BF16)

                    if half == 1:
                        own[u, piece(r), c] = product

    def run_z1(u, r):
        @pl.when(depth == 0)
        def _():
            if len(paced) >= WINDOW:
                cross_copy(*paced[-WINDOW]).wait_send()
            send_inward(u, r)

        paced.append((u, r))

        @pl.when(not_end)
        def _():
            up_copy(u, r).wait_recv()
            a = piece(r)
            total = own[u, a, :] + up[u, a, :].astype(F32)
            own[u, a, :] = total
            up[u, a, :] = total.astype(BF16)
            send_inward(u, r)

    def run_z2(u, r):
        @pl.when(inner)
        def _():
            cross_copy(u, r).wait_recv()
            a = piece(r)
            image[u, a, :] = (own[u, a, :] + image[u, a, :].astype(F32)).astype(BF16)

            @pl.when(not_end)
            def _():
                down_copy(u, r).start()

    def run_z3(u, r):
        if half > 2:
            @pl.when(jnp.logical_and(not_end, jnp.logical_not(inner)))
            def _():
                down_copy(u, r).wait_recv()
                down_copy(u, r).start()

    def run_m1():
        for f in range(2):
            total = squares[f, :, :128]
            for j in range(1, width // 128):
                total = total + squares[f, :, j * 128 : (j + 1) * 128]
            means[col, f] = total
        for d in range(1, n_col):
            mean_copy(d).start()

    def run_m2():
        for d in range(1, n_col):
            mean_arrival(d).wait_recv()
        entries = chunks * tokens * width * n_col
        for f in range(2):
            total = means[0, f]
            for j in range(1, n_col):
                total = total + means[j, f]
            scale[1 - f] = gram_scale / (chunks * tokens) * (jnp.sum(total) / entries)

    def change(f, r):
        if half > 1:
            @pl.when(depth == 0)
            def _():
                for u in range(f * chunks, (f + 1) * chunks):
                    down_copy(u, r).wait_recv()

        @pl.loop(0, width // step)
        def _(j):
            c = at(j * step, step, step)
            total = None
            for u in range(f * chunks, (f + 1) * chunks):
                term = jnp.dot(image[u, piece(r), :], proj[u, :, c], preferred_element_type=F32)
                total = term if total is None else total + term
            k_v[f, piece(r), c] = (
                keep_scale * k_v[f, piece(r), c].astype(F32) - scale[f] * total
            ).astype(BF16)

    def run_f(f, r):
        if f == 0:
            @pl.loop(0, pieces)
            def _(i):
                change(0, i)

            copy = pltpu.make_async_copy(k_v.at[0], outs[0], store_sem.at[pieces])
        else:
            change(1, r)
            copy = pltpu.make_async_copy(k_v.at[1, piece(r)], outs[1].at[piece(r)], store_sem.at[r])
        copy.start()
        stores.append(copy)

    squares[...] = jnp.zeros(squares.shape, F32)
    for event in order:
        kind = event[0]
        if kind == "S":
            run_squares(event[1])
        elif kind == "E":
            run_e(event[1], event[2])
        elif kind == "Z0":
            run_z0(event[1])
        elif kind == "Z1":
            run_z1(*event[1:])
        elif kind == "Z2":
            run_z2(*event[1:])
        elif kind == "Z3":
            run_z3(*event[1:])
        elif kind == "M1":
            run_m1()
        elif kind == "M2":
            run_m2()
        elif kind == "F0":
            run_f(0, None)
        else:
            run_f(1, event[1])

    for u in range(units):
        for s in range(levels):
            scatter_copy(u, s).wait_send()
            gather_copy(u, s).wait_send()

    for i, (u, r) in enumerate(paced):
        if i + WINDOW >= len(paced):
            cross_copy(u, r).wait_send()
        else:
            @pl.when(not_end)
            def _(u=u, r=r):
                cross_copy(u, r).wait_send()

        @pl.when(not_end)
        def _(u=u, r=r):
            down_copy(u, r).wait_send()
    for d in range(1, n_col):
        mean_copy(d).wait_send()
    for copy in stores:
        copy.wait()


def local(n_row, n_col, activations, cotangents, act_factor, grad_factor):
    rows, width = act_factor.shape
    tokens = activations.shape[0] // CHUNKS
    units = 2 * CHUNKS
    levels = n_row.bit_length() - 1
    order = schedule(levels, units, PIECES, n_col // 2, tokens, rows, width)
    dma = pltpu.SemaphoreType.DMA
    anywhere = pl.BlockSpec(memory_space=pl.ANY)
    return pl.pallas_call(
        functools.partial(kernel, n_row, n_col, order, CHUNKS, PIECES),
        out_shape=[jax.ShapeDtypeStruct((rows, width), BF16)] * 2,
        in_specs=[anywhere] * 4,
        out_specs=[anywhere] * 2,
        scratch_shapes=[
            pltpu.VMEM((2,) + activations.shape, BF16),
            pltpu.VMEM((2, rows, width), BF16),
            pltpu.VMEM((units, tokens // 2, width), F32),
            pltpu.VMEM((units, tokens, width), BF16),
            pltpu.VMEM((units, rows, tokens), F32),
            pltpu.VMEM((units, rows, tokens), BF16),
            pltpu.VMEM((units, rows, tokens), BF16),
            pltpu.VMEM((2, 8, width), F32),
            pltpu.VMEM((n_col, 2, 8, 128), F32),
        ]
        + [pltpu.VMEM((units, tokens >> (s + 1), width), BF16) for s in range(levels)] * 2
        + [
            dma((2, 2)),
            dma((PIECES + 1,)),
            dma((units, 2 * levels)),
            dma((units, 2 * levels)),
            dma((units, PIECES)),
            dma((units, PIECES)),
            dma((units, PIECES)),
            dma((units, PIECES)),
            dma((n_col,)),
            dma((n_col,)),
        ],
        compiler_params=pltpu.CompilerParams(
            collective_id=0, has_side_effects=True, vmem_limit_bytes=67043328
        ),
    )(activations, cotangents, act_factor, grad_factor)


def solution(mesh):
    return jax.shard_map(
        functools.partial(local, mesh.shape["row"], mesh.shape["col"]),
        mesh=mesh,
        in_specs=(P(None, "row"), P(None, "row"), P("row", "col"), P("row", "col")),
        out_specs=(P("row", "col"), P("row", "col")),
        check_vma=False,
    )
```
